32 devices in a mesh: shard: 2 (over core), ctx: 4 (over y, x), tp: 4 (over z).
Axes of the slice: x: 2, y: 2, z: 4, core: 2. Of those that a mesh axis runs over, the one named last changes fastest.
Arguments:
- hidden_in: bfloat16 [2, 1024, 640], P('shard', ('ctx', 'tp')), may hold values from -6 to 6
- positions: int32 [2, 1024], P('shard', 'ctx'), may hold values from 0 to 1023, as said below
- cotangent: bfloat16 [2, 1024, 640], P('shard', ('ctx', 'tp')), may hold values from -6 to 6
- input_gain: bfloat16 [640], P('shard'), may hold values from 0.5 to 1.5
- query_weight: bfloat16 [640, 1024], P('shard', 'tp'), may hold values from -0.25 to 0.25
- key_weight: bfloat16 [640, 256], P('shard'), may hold values from -0.25 to 0.25
- value_weight: bfloat16 [640, 256], P('shard'), may hold values from -0.25 to 0.25
- query_gain: bfloat16 [256], P('shard'), may hold values from 0.5 to 1.5
- key_gain: bfloat16 [256], P('shard'), may hold values from 0.5 to 1.5
- out_weight: bfloat16 [1024, 640], P('tp', 'shard'), may hold values from -0.1875 to 0.1875
- attn_post_gain: bfloat16 [640], P('shard'), may hold values from 0.5 to 1.5
- ffn_pre_gain: bfloat16 [640], P('shard'), may hold values from 0.5 to 1.5
- gate_weight: bfloat16 [640, 2048], P('shard', 'tp'), may hold values from -0.25 to 0.25
- up_weight: bfloat16 [640, 2048], P('shard', 'tp'), may hold values from -0.25 to 0.25
- down_weight: bfloat16 [2048, 640], P('tp', 'shard'), may hold values from -0.125 to 0.125
- ffn_post_gain: bfloat16 [640], P('shard'), may hold values from 0.5 to 1.5
Outputs:
- block_out: float32 [2, 1024, 640], P('shard', ('ctx', 'tp'))
- hidden_grad: float32 [2, 1024, 640], P('shard', ('ctx', 'tp'))
- input_gain_grad: float32 [640], P('shard')
- query_weight_grad: float32 [640, 1024], P('shard', 'tp')
- key_weight_grad: float32 [640, 256], P('shard')
- value_weight_grad: float32 [640, 256], P('shard')
- query_gain_grad: float32 [256], P('shard')
- key_gain_grad: float32 [256], P('shard')
- out_weight_grad: float32 [1024, 640], P('tp', 'shard')
- attn_post_gain_grad: float32 [640], P('shard')
- ffn_pre_gain_grad: float32 [640], P('shard')
- gate_weight_grad: float32 [640, 2048], P('shard', 'tp')
- up_weight_grad: float32 [640, 2048], P('shard', 'tp')
- down_weight_grad: float32 [2048, 640], P('tp', 'shard')
- ffn_post_gain_grad: float32 [640], P('shard')
The draws below stay inside these ranges and needn't reach their ends.
Inputs may be any that keep to these rules, and one draw needn't show every extreme that they name: Within each sequence the positions are each of 0 to 1023 once, laid out in aligned blocks of 64 tokens that hold 64 consecutive positions in increasing order; the order of the blocks is arbitrary.
All inputs are finite; a program needn't handle non-finite values.
Results may differ from the reference program's by a relative error of at most 0.023.
Values may be sent and summed in bfloat16 or wider, within the bound.
No kernel may reach another device: no remote copies, remote signals or barrier semaphores. Data moves between devices by JAX's collectives and lax.ppermute only.
A program may use at most 64 MiB of HBM per device.

```python
import math
import jax
import jax.numpy as jnp
from jax import lax

D = 640
H = 4
HD = 256
FF = 2048
LEN = 1024
BLK = 64
SEQS = 2


def draw_positions(key, part):
    blocks = LEN // BLK
    keys = jax.random.split(jax.random.fold_in(key, 7), SEQS)
    orders = jax.vmap(lambda single: jax.random.permutation(single, blocks))(keys)
    places = orders[:, :, None] * BLK + jnp.arange(BLK, dtype=jnp.int32)[None, None, :]
    return places.reshape(SEQS, LEN).astype(jnp.int32)


def level_of(key, extent, cuts, low, high):
    gain = 1.0
    for position, shards_of in cuts:
        steps = jax.random.uniform(jax.random.fold_in(jax.random.fold_in(key, 6), position), (shards_of,), jnp.float32, low / len(cuts), high / len(cuts))
        gain = gain * jnp.repeat(jnp.exp(steps), extent[position] // shards_of).reshape((-1,) + (1,) * (len(extent) - 1 - position))
    return gain


def noise(own_key, dims, deviation, most, shards=(), kind=jnp.bfloat16):
    entries = jax.random.normal(own_key, dims, jnp.float32) * deviation
    if len(shards) > 0:
        entries = level_of(own_key, dims, shards, -0.22, 0.18) * entries
    return jnp.clip(entries, min=-most, max=most).astype(kind)


def setup_inputs(seed: int = 0) -> dict:
    key_list = jax.random.split(jax.random.key(seed), 17)
    return {
        "hidden_in": noise(key_list[0], (SEQS, LEN, D), 1.0, 6.0, ((0, 2), (1, 16))),
        "positions": draw_positions(jax.random.fold_in(key_list[16], 71), 0),
        "cotangent": noise(key_list[2], (SEQS, LEN, D), 1.0, 6.0, ((0, 2), (1, 16))),
        "input_gain": jnp.clip(1.0 + 0.1 * jax.random.normal(key_list[3], (D,), jnp.float32), 0.5, 1.5).astype(jnp.bfloat16),
        "query_weight": noise(key_list[4], (D, H * HD), D ** -0.5, 0.25, ((0, 2), (1, 4))),
        "key_weight": noise(key_list[5], (D, HD), D ** -0.5, 0.25, ((0, 2),)),
        "value_weight": noise(key_list[6], (D, HD), D ** -0.5, 0.25, ((0, 2),)),
        "query_gain": jnp.clip(1.0 + 0.1 * jax.random.normal(key_list[7], (HD,), jnp.float32), 0.5, 1.5).astype(jnp.bfloat16),
        "key_gain": jnp.clip(1.0 + 0.1 * jax.random.normal(key_list[8], (HD,), jnp.float32), 0.5, 1.5).astype(jnp.bfloat16),
        "out_weight": noise(key_list[9], (H * HD, D), (H * HD) ** -0.5, 0.1875, ((0, 4), (1, 2))),
        "attn_post_gain": jnp.clip(1.0 + 0.1 * jax.random.normal(key_list[10], (D,), jnp.float32), 0.5, 1.5).astype(jnp.bfloat16),
        "ffn_pre_gain": jnp.clip(1.0 + 0.1 * jax.random.normal(key_list[11], (D,), jnp.float32), 0.5, 1.5).astype(jnp.bfloat16),
        "gate_weight": noise(key_list[12], (D, FF), D ** -0.5, 0.25, ((0, 2), (1, 4))),
        "up_weight": noise(key_list[13], (D, FF), D ** -0.5, 0.25, ((0, 2), (1, 4))),
        "down_weight": noise(key_list[14], (FF, D), FF ** -0.5, 0.125, ((0, 4), (1, 2))),
        "ffn_post_gain": jnp.clip(1.0 + 0.1 * jax.random.normal(key_list[15], (D,), jnp.float32), 0.5, 1.5).astype(jnp.bfloat16),
    }


epsilon = 1e-06
rope_base = 1000000.0
gelu_coef = 0.044715

def rms_scale(value):
    return lax.rsqrt(lax.optimization_barrier(jnp.mean(value * value, axis=-1, keepdims=True)) + epsilon)

def norm_back(grad_unit, unit, scale):
    return scale * (grad_unit - unit * lax.optimization_barrier(jnp.mean(grad_unit * unit, axis=-1, keepdims=True)))

def gelu_pair(value):
    root = math.sqrt(2.0 / math.pi)
    tangent = jnp.tanh(root * (value + gelu_coef * value * value * value))
    result = 0.5 * value * (1.0 + tangent)
    slope = 0.5 * (1.0 + tangent) + 0.5 * value * (1.0 - tangent * tangent) * root * (1.0 + 3.0 * gelu_coef * value * value)
    return (result, slope)

def rope_tables(places, width):
    half = width // 2
    freqs = rope_base ** (-(jnp.arange(half, dtype=jnp.float32) * 2.0 / width))
    angles = places.astype(jnp.float32)[:, None] * freqs[None, :]
    return (jnp.cos(angles)[:, None, :], jnp.sin(angles)[:, None, :])

def rotate(value, cosine, sine):
    half = value.shape[-1] // 2
    first = value[..., :half]
    second = value[..., half:]
    return jnp.concatenate([first * cosine - second * sine, second * cosine + first * sine], axis=-1)

def unrotate(value, cosine, sine):
    half = value.shape[-1] // 2
    first = value[..., :half]
    second = value[..., half:]
    return jnp.concatenate([first * cosine + second * sine, second * cosine - first * sine], axis=-1)

def sequence_pass(weights, tokens, places, upstream):
    input_gain, query_weight, key_weight, value_weight, query_gain, key_gain, out_weight, attn_post_gain, ffn_pre_gain, gate_weight, up_weight, down_weight, ffn_post_gain = weights
    in_gain = input_gain.astype(jnp.float32)
    qgain = query_gain.astype(jnp.float32)
    kgain = key_gain.astype(jnp.float32)
    post_gain = attn_post_gain.astype(jnp.float32)
    pre_gain = ffn_pre_gain.astype(jnp.float32)
    last_gain = ffn_post_gain.astype(jnp.float32)
    count = tokens.shape[0]
    factor = 1.0 / math.sqrt(HD)
    rows = tokens.astype(jnp.float32)
    scale_in = rms_scale(rows)
    unit_in = rows * scale_in
    normed_in = (unit_in * in_gain).astype(jnp.bfloat16)
    query_raw = jnp.dot(normed_in, query_weight, preferred_element_type=jnp.float32).reshape(count, H, HD)
    query_scale = rms_scale(query_raw)
    query_unit = query_raw * query_scale
    key_raw = jnp.dot(normed_in, key_weight, preferred_element_type=jnp.float32)
    key_scale = rms_scale(key_raw)
    key_unit = key_raw * key_scale
    values = jnp.dot(normed_in, value_weight, preferred_element_type=jnp.float32).astype(jnp.bfloat16)
    cosine, sine = rope_tables(places, HD)
    query_rot = rotate(query_unit * qgain, cosine, sine).astype(jnp.bfloat16)
    key_rot = rotate((key_unit * kgain)[:, None, :], cosine, sine)[:, 0].astype(jnp.bfloat16)
    visible = places[None, None, :] <= places[None, :, None]
    scores = jnp.einsum('qhd,kd->hqk', query_rot.astype(jnp.float32), key_rot.astype(jnp.float32)) * factor
    scores = jnp.where(visible, scores, -1e+30)
    logsum = jnp.log(lax.optimization_barrier(jnp.sum(jnp.exp(scores), axis=-1, keepdims=True)))
    probs_full = jnp.exp(scores - logsum)
    probs = probs_full.astype(jnp.bfloat16)
    context3 = jnp.einsum('hqk,kd->qhd', probs.astype(jnp.float32), values.astype(jnp.float32)).astype(jnp.bfloat16)
    context = context3.reshape(count, H * HD)
    attn_proj = jnp.dot(context, out_weight, preferred_element_type=jnp.float32)
    attn_scale = rms_scale(attn_proj)
    attn_unit = attn_proj * attn_scale
    resid = rows + attn_unit * post_gain
    ffn_scale = rms_scale(resid)
    ffn_unit = resid * ffn_scale
    ffn_in = (ffn_unit * pre_gain).astype(jnp.bfloat16)
    gate = jnp.dot(ffn_in, gate_weight, preferred_element_type=jnp.float32)
    upper = jnp.dot(ffn_in, up_weight, preferred_element_type=jnp.float32)
    gelu_val, gelu_slope = gelu_pair(gate)
    hidden_act = (gelu_val * upper).astype(jnp.bfloat16)
    ffn_proj = jnp.dot(hidden_act, down_weight, preferred_element_type=jnp.float32)
    out_scale = rms_scale(ffn_proj)
    out_unit = ffn_proj * out_scale
    block_out = resid + out_unit * last_gain
    grad_out = upstream.astype(jnp.float32)
    last_gain_grad = lax.optimization_barrier(jnp.sum(grad_out * out_unit, axis=0))
    grad_ffn_proj = norm_back(grad_out * last_gain, out_unit, out_scale).astype(jnp.bfloat16)
    down_grad = jnp.dot(hidden_act.T, grad_ffn_proj, preferred_element_type=jnp.float32)
    grad_hidden = jnp.dot(grad_ffn_proj, down_weight.T, preferred_element_type=jnp.float32)
    grad_up = (grad_hidden * gelu_val).astype(jnp.bfloat16)
    grad_gate = (grad_hidden * upper * gelu_slope).astype(jnp.bfloat16)
    gate_grad = jnp.dot(ffn_in.T, grad_gate, preferred_element_type=jnp.float32)
    up_grad = jnp.dot(ffn_in.T, grad_up, preferred_element_type=jnp.float32)
    grad_ffn_in = jnp.dot(grad_gate, gate_weight.T, preferred_element_type=jnp.float32) + jnp.dot(grad_up, up_weight.T, preferred_element_type=jnp.float32)
    pre_gain_grad = lax.optimization_barrier(jnp.sum(grad_ffn_in * ffn_unit, axis=0))
    grad_resid = grad_out + norm_back(grad_ffn_in * pre_gain, ffn_unit, ffn_scale)
    post_gain_grad = lax.optimization_barrier(jnp.sum(grad_resid * attn_unit, axis=0))
    grad_attn = norm_back(grad_resid * post_gain, attn_unit, attn_scale).astype(jnp.bfloat16)
    out_grad = jnp.dot(context.T, grad_attn, preferred_element_type=jnp.float32)
    grad_context = jnp.dot(grad_attn, out_weight.T, preferred_element_type=jnp.float32).astype(jnp.bfloat16).reshape(count, H, HD)
    delta = lax.optimization_barrier(jnp.sum(grad_context.astype(jnp.float32) * context3.astype(jnp.float32), axis=-1))
    grad_probs = jnp.einsum('qhd,kd->hqk', grad_context.astype(jnp.float32), values.astype(jnp.float32))
    grad_scores = (probs_full * (grad_probs - delta.T[:, :, None]) * factor).astype(jnp.bfloat16)
    grad_query_rot = jnp.einsum('hqk,kd->qhd', grad_scores.astype(jnp.float32), key_rot.astype(jnp.float32))
    grad_key_rot = jnp.einsum('hqk,qhd->kd', grad_scores.astype(jnp.float32), query_rot.astype(jnp.float32))
    grad_values = jnp.einsum('hqk,qhd->kd', probs.astype(jnp.float32), grad_context.astype(jnp.float32))
    grad_query_gained = unrotate(grad_query_rot, cosine, sine)
    grad_key_gained = unrotate(grad_key_rot[:, None, :], cosine, sine)[:, 0]
    qgain_grad = lax.optimization_barrier(jnp.sum(grad_query_gained * query_unit, axis=(0, 1)))
    kgain_grad = lax.optimization_barrier(jnp.sum(grad_key_gained * key_unit, axis=0))
    grad_query = norm_back(grad_query_gained * qgain, query_unit, query_scale).astype(jnp.bfloat16).reshape(count, H * HD)
    grad_key = norm_back(grad_key_gained * kgain, key_unit, key_scale).astype(jnp.bfloat16)
    grad_value_low = grad_values.astype(jnp.bfloat16)
    query_grad = jnp.dot(normed_in.T, grad_query, preferred_element_type=jnp.float32)
    key_grad = jnp.dot(normed_in.T, grad_key, preferred_element_type=jnp.float32)
    value_grad = jnp.dot(normed_in.T, grad_value_low, preferred_element_type=jnp.float32)
    grad_normed = jnp.dot(grad_query, query_weight.T, preferred_element_type=jnp.float32) + jnp.dot(grad_key, key_weight.T, preferred_element_type=jnp.float32) + jnp.dot(grad_value_low, value_weight.T, preferred_element_type=jnp.float32)
    in_gain_grad = lax.optimization_barrier(jnp.sum(grad_normed * unit_in, axis=0))
    hidden_grad = grad_resid + norm_back(grad_normed * in_gain, unit_in, scale_in)
    grads = (in_gain_grad, query_grad, key_grad, value_grad, qgain_grad, kgain_grad, out_grad, post_gain_grad, pre_gain_grad, gate_grad, up_grad, down_grad, last_gain_grad)
    return (block_out, hidden_grad, grads)

def reference(hidden_in, positions, cotangent, input_gain, query_weight, key_weight, value_weight, query_gain, key_gain, out_weight, attn_post_gain, ffn_pre_gain, gate_weight, up_weight, down_weight, ffn_post_gain):
    weights = (input_gain, query_weight, key_weight, value_weight, query_gain, key_gain, out_weight, attn_post_gain, ffn_pre_gain, gate_weight, up_weight, down_weight, ffn_post_gain)

    def advance(carry, item):
        block_out, hidden_grad, grads = sequence_pass(weights, item[0], item[1], item[2])
        return (tuple((left + right for left, right in zip(carry, grads))), (block_out, hidden_grad))
    start = tuple((jnp.zeros(weight.shape, jnp.float32) for weight in weights))
    totals, outputs = lax.scan(advance, start, (hidden_in, positions, cotangent))
    return (outputs[0], outputs[1], totals[0], totals[1], totals[2], totals[3], totals[4], totals[5], totals[6], totals[7], totals[8], totals[9], totals[10], totals[11], totals[12])
```

```python
import math

import jax
import jax.numpy as jnp
from jax import lax
from jax.sharding import PartitionSpec as P

epsilon = 1e-06
rope_base = 1000000.0
gelu_coef = 0.044715
low = jnp.bfloat16
full = jnp.float32


def rms_scale(value):
    return lax.rsqrt(jnp.mean(value * value, axis=-1, keepdims=True) + epsilon)


def norm_back(grad_unit, unit, scale):
    return scale * (grad_unit - unit * jnp.mean(grad_unit * unit, axis=-1, keepdims=True))


def gelu_pair(value):
    root = math.sqrt(2.0 / math.pi)
    tangent = jnp.tanh(root * (value + gelu_coef * value * value * value))
    result = 0.5 * value * (1.0 + tangent)
    slope = 0.5 * (1.0 + tangent) + 0.5 * value * (1.0 - tangent * tangent) * root * (
        1.0 + 3.0 * gelu_coef * value * value
    )
    return (result, slope)


def rope_tables(places, width):
    half = width // 2
    freqs = rope_base ** (-(jnp.arange(half, dtype=full) * 2.0 / width))
    angles = places.astype(full)[:, None] * freqs[None, :]
    return (jnp.cos(angles), jnp.sin(angles))


def rotate(value, cosine, sine):
    half = value.shape[-1] // 2
    first = value[..., :half]
    second = value[..., half:]
    return jnp.concatenate(
        [first * cosine - second * sine, second * cosine + first * sine], axis=-1
    )


def unrotate(value, cosine, sine):
    return rotate(value, cosine, -sine)


def dot(left, right):
    return jnp.dot(left, right, preferred_element_type=full)


def dot_tn(left, right):
    return lax.dot_general(left, right, (((0,), (0,)), ((), ())), preferred_element_type=full)


def dot_nt(left, right):
    return lax.dot_general(left, right, (((1,), (1,)), ((), ())), preferred_element_type=full)


def pieces(value, axis):
    count = lax.axis_size(axis)
    return [value] + [
        lax.ppermute(value, axis, [(i, (i + o) % count) for i in range(count)])
        for o in range(1, count)
    ]


def gather_rows(value, axis):
    return jnp.concatenate(pieces(value, axis), axis=0)


def scatter_rows(value, axis):
    count = lax.axis_size(axis)
    rows = value.shape[0] // count
    total = value[:rows].astype(full)
    sent = value.astype(low)
    for o in range(1, count):
        block = sent[o * rows : (o + 1) * rows]
        total = total + lax.ppermute(
            block, axis, [(i, (i - o) % count) for i in range(count)]
        ).astype(full)
    return total


def shard_gather(value, dim):
    count = lax.axis_size("shard")
    if count != 2:
        return lax.all_gather(value, "shard", axis=dim, tiled=True)
    other = lax.ppermute(value, "shard", [(0, 1), (1, 0)])
    first = lax.axis_index("shard") == 0
    return jnp.concatenate(
        [jnp.where(first, value, other), jnp.where(first, other, value)], axis=dim
    )


def shard_scatter(value):
    count = lax.axis_size("shard")
    if count != 2:
        return lax.psum_scatter(value.astype(low), "shard", scatter_dimension=0, tiled=True)
    rows = value.shape[0] // 2
    me = lax.axis_index("shard")
    theirs = lax.dynamic_slice_in_dim(value, (1 - me) * rows, rows, 0).astype(low)
    mine = lax.dynamic_slice_in_dim(value, me * rows, rows, 0)
    return (
        mine.astype(full) + lax.ppermute(theirs, "shard", [(0, 1), (1, 0)]).astype(full)
    ).astype(low)


def axis_total(value, axis):
    count = lax.axis_size(axis)
    rows = value.shape[0] // count
    me = lax.axis_index(axis)
    total = None
    for o in range(count):
        block = lax.dynamic_slice_in_dim(value, ((me + o) % count) * rows, rows, 0)
        if o == 0:
            total = block.astype(full)
        else:
            total = total + lax.ppermute(
                block, axis, [(i, (i + o) % count) for i in range(count)]
            ).astype(full)
    return total.astype(low)


def axis_fill(chunk, axis):
    count = lax.axis_size(axis)
    rows = chunk.shape[0]
    me = lax.axis_index(axis)
    held = [chunk] + [
        lax.ppermute(chunk, axis, [(i, (i - o) % count) for i in range(count)])
        for o in range(1, count)
    ]
    twice = jnp.concatenate(held + held, axis=0)
    start = ((count - me) % count) * rows
    return lax.dynamic_slice_in_dim(twice, start, rows * count, 0)


def axis_sum(value, axis):
    total = None
    for piece in pieces(value, axis):
        total = piece.astype(full) if total is None else total + piece.astype(full)
    return total


def body(
    hidden_in,
    positions,
    cotangent,
    input_gain,
    query_weight,
    key_weight,
    value_weight,
    query_gain,
    key_gain,
    out_weight,
    attn_post_gain,
    ffn_pre_gain,
    gate_weight,
    up_weight,
    down_weight,
    ffn_post_gain,
):
    width = hidden_in.shape[-1]
    head_dim = key_weight.shape[1]
    head_cols = query_weight.shape[1]
    hidden_cols = gate_weight.shape[1]
    heads = head_cols // head_dim
    factor = 1.0 / math.sqrt(head_dim)
    shards = lax.axis_size("shard")
    tps = lax.axis_size("tp")
    ctxs = lax.axis_size("ctx")
    own_in = hidden_in.reshape(-1, width)
    own_cot = cotangent.reshape(-1, width)
    part_rows = own_in.shape[0]
    me_tp = lax.axis_index("tp")

    rows_low = gather_rows(own_in, "tp")
    count = rows_low.shape[0]
    natural = positions.reshape(tps, part_rows)
    places = jnp.concatenate(
        [
            lax.dynamic_slice_in_dim(natural, (me_tp - o) % tps, 1, 0).reshape(-1)
            for o in range(tps)
        ]
    )
    places_all = gather_rows(places, "ctx")

    wide = width // shards
    slim = head_dim // shards
    packed = jnp.concatenate(
        [input_gain, attn_post_gain, ffn_pre_gain, ffn_post_gain, query_gain, key_gain]
    ).reshape(1, -1)
    gains = shard_gather(packed, 0).astype(full)

    def gain_at(start, size):
        return gains[:, start : start + size].reshape(-1)

    in_gain = gain_at(0, wide)
    post_gain = gain_at(wide, wide)
    pre_gain = gain_at(2 * wide, wide)
    last_gain = gain_at(3 * wide, wide)
    qgain = gain_at(4 * wide, slim)
    kgain = gain_at(4 * wide + slim, slim)
    qkv_full = shard_gather(jnp.concatenate([query_weight, key_weight, value_weight], axis=1), 0)
    query_full = qkv_full[:, :head_cols]
    key_full = qkv_full[:, head_cols : head_cols + head_dim]
    value_full = qkv_full[:, head_cols + head_dim :]
    out_full = shard_gather(out_weight, 1)
    gate_full = shard_gather(gate_weight, 0)
    up_full = shard_gather(up_weight, 0)
    down_full = shard_gather(down_weight, 1)

    rows = rows_low.astype(full)
    scale_in = rms_scale(rows)
    unit_in = rows * scale_in
    normed_in = (unit_in * in_gain).astype(low)
    cosine, sine = rope_tables(places, head_dim)
    key_raw = dot(normed_in, key_full)
    key_scale = rms_scale(key_raw)
    key_unit = key_raw * key_scale
    key_rot = rotate(key_unit * kgain, cosine, sine).astype(low)
    key_all = gather_rows(key_rot, "ctx")
    values = dot(normed_in, value_full).astype(low)
    value_all = gather_rows(values, "ctx")
    query_raw = dot(normed_in, query_full).reshape(count, heads, head_dim)
    query_scale = rms_scale(query_raw)
    query_unit = query_raw * query_scale
    query_rot = rotate(query_unit * qgain, cosine[:, None, :], sine[:, None, :]).astype(low)
    visible = places_all[None, None, :] <= places[None, :, None]
    scores = (
        jnp.einsum("qhd,kd->hqk", query_rot, key_all, preferred_element_type=full) * factor
    )
    weight = jnp.exp(jnp.where(visible, scores, -1e30))
    probs_full = weight * (1.0 / jnp.sum(weight, axis=-1, keepdims=True))
    probs = probs_full.astype(low)
    context3 = jnp.einsum(
        "hqk,kd->qhd", probs, value_all, preferred_element_type=full
    ).astype(low)
    context = context3.reshape(count, head_cols)
    attn_proj = scatter_rows(dot(context, out_full), "tp")

    own_rows = own_in.astype(full)
    grad_out = own_cot.astype(full)
    attn_scale = rms_scale(attn_proj)
    attn_unit = attn_proj * attn_scale
    resid = own_rows + attn_unit * post_gain
    ffn_scale = rms_scale(resid)
    ffn_unit = resid * ffn_scale
    ffn_rows = gather_rows((ffn_unit * pre_gain).astype(low), "tp")

    gate = dot(ffn_rows, gate_full)
    upper = dot(ffn_rows, up_full)
    gelu_val, gelu_slope = gelu_pair(gate)
    hidden_act = (gelu_val * upper).astype(low)
    ffn_proj = scatter_rows(dot(hidden_act, down_full), "tp")

    out_scale = rms_scale(ffn_proj)
    out_unit = ffn_proj * out_scale
    block_out = resid + out_unit * last_gain
    last_gain_grad = jnp.sum(grad_out * out_unit, axis=0)
    grad_proj_own = norm_back(grad_out * last_gain, out_unit, out_scale).astype(low)
    grad_proj_rows = gather_rows(grad_proj_own, "tp")

    grad_hidden = dot_nt(grad_proj_rows, down_full)
    grad_up = (grad_hidden * gelu_val).astype(low)
    grad_gate = (grad_hidden * upper * gelu_slope).astype(low)
    grad_ffn_in = scatter_rows(dot_nt(grad_gate, gate_full) + dot_nt(grad_up, up_full), "tp")

    pre_gain_grad = jnp.sum(grad_ffn_in * ffn_unit, axis=0)
    grad_resid = grad_out + norm_back(grad_ffn_in * pre_gain, ffn_unit, ffn_scale)
    post_gain_grad = jnp.sum(grad_resid * attn_unit, axis=0)
    grad_attn_own = norm_back(grad_resid * post_gain, attn_unit, attn_scale).astype(low)
    grad_attn_rows = gather_rows(grad_attn_own, "tp")

    early = shard_scatter(
        jnp.concatenate(
            [
                dot_tn(ffn_rows, grad_gate).astype(low),
                dot_tn(ffn_rows, grad_up).astype(low),
                dot_tn(grad_proj_rows, hidden_act).astype(low),
            ],
            axis=1,
        )
    )
    early_all = axis_fill(axis_total(early, "ctx"), "ctx")

    grad_context_flat = dot_nt(grad_attn_rows, out_full).astype(low)
    grad_context = grad_context_flat.reshape(count, heads, head_dim)
    delta = jnp.sum(grad_context.astype(full) * context3.astype(full), axis=-1)
    grad_probs = jnp.einsum("qhd,kd->hqk", grad_context, value_all, preferred_element_type=full)
    grad_scores = (probs_full * (grad_probs - delta.T[:, :, None]) * factor).astype(low)
    grad_key_part = jnp.einsum(
        "hqk,qhd->kd", grad_scores, query_rot, preferred_element_type=full
    ).astype(low)
    grad_value_part = jnp.einsum(
        "hqk,qhd->kd", probs, grad_context, preferred_element_type=full
    ).astype(low)
    grad_query_rot = jnp.einsum("hqk,kd->qhd", grad_scores, key_all, preferred_element_type=full)
    both = scatter_rows(jnp.concatenate([grad_key_part, grad_value_part], axis=1), "ctx")
    grad_key_rot = both[:, :head_dim]
    grad_value_low = both[:, head_dim:].astype(low)

    grad_query_gained = unrotate(grad_query_rot, cosine[:, None, :], sine[:, None, :])
    qgain_grad = jnp.sum(grad_query_gained * query_unit, axis=(0, 1))
    grad_query = (
        norm_back(grad_query_gained * qgain, query_unit, query_scale)
        .astype(low)
        .reshape(count, head_cols)
    )
    query_part = dot_nt(grad_query, query_full)

    grad_key_gained = unrotate(grad_key_rot, cosine, sine)
    kgain_grad = jnp.sum(grad_key_gained * key_unit, axis=0)
    grad_key = norm_back(grad_key_gained * kgain, key_unit, key_scale).astype(low)
    grad_normed_part = (
        query_part + dot_nt(grad_key, key_full) + dot_nt(grad_value_low, value_full)
    )
    in_gain_grad = jnp.sum(grad_normed_part * unit_in, axis=0)
    grad_normed = scatter_rows(grad_normed_part, "tp")
    own_scale = rms_scale(own_rows)
    hidden_grad = grad_resid + norm_back(grad_normed * in_gain, own_rows * own_scale, own_scale)

    small_width = 2 * head_dim
    late_q = jnp.concatenate(
        [
            dot_tn(normed_in, grad_query).astype(low),
            dot_tn(grad_attn_rows, context).astype(low),
        ],
        axis=1,
    )
    late_kv = jnp.concatenate(
        [
            dot_tn(normed_in, grad_key).astype(low),
            dot_tn(normed_in, grad_value_low).astype(low),
        ],
        axis=1,
    )
    vectors = jnp.concatenate(
        [
            item.reshape(shards, -1)
            for item in (
                in_gain_grad,
                post_gain_grad,
                pre_gain_grad,
                last_gain_grad,
                qgain_grad,
                kgain_grad,
            )
        ],
        axis=1,
    ).astype(low)
    length = vectors.shape[1]
    late_q_own = axis_total(shard_scatter(late_q), "ctx")
    late_kv_own = axis_total(shard_scatter(late_kv), "ctx")
    late_kv_own = axis_sum(late_kv_own, "tp").astype(low)
    late_all = axis_fill(jnp.concatenate([late_q_own, late_kv_own], axis=1), "ctx").astype(full)
    vector_own = shard_scatter(vectors.reshape(shards, 1, length)).reshape(1, length)
    vector_own = axis_sum(axis_sum(vector_own, "ctx").astype(low), "tp").reshape(length)

    def vector_at(start, size):
        return vector_own[start : start + size]

    early_all = early_all.astype(full)
    gate_grad = early_all[:, :hidden_cols]
    up_grad = early_all[:, hidden_cols : 2 * hidden_cols]
    down_grad = early_all[:, 2 * hidden_cols :].T
    query_grad = late_all[:, :head_cols]
    out_grad = late_all[:, head_cols : 2 * head_cols].T
    key_grad = late_all[:, 2 * head_cols : 2 * head_cols + head_dim]
    value_grad = late_all[:, 2 * head_cols + head_dim :]
    return (
        block_out.reshape(hidden_in.shape),
        hidden_grad.reshape(hidden_in.shape),
        vector_at(0, wide),
        query_grad,
        key_grad,
        value_grad,
        vector_at(4 * wide, slim),
        vector_at(4 * wide + slim, slim),
        out_grad,
        vector_at(wide, wide),
        vector_at(2 * wide, wide),
        gate_grad,
        up_grad,
        down_grad,
        vector_at(3 * wide, wide),
    )


def solution(mesh):
    placed = (
        P("shard", ("ctx", "tp"), None),
        P("shard", "ctx"),
        P("shard", ("ctx", "tp"), None),
        P("shard"),
        P("shard", "tp"),
        P("shard", None),
        P("shard", None),
        P("shard"),
        P("shard"),
        P("tp", "shard"),
        P("shard"),
        P("shard"),
        P("shard", "tp"),
        P("shard", "tp"),
        P("tp", "shard"),
        P("shard"),
    )
    return jax.shard_map(
        body,
        mesh=mesh,
        in_specs=placed,
        out_specs=(
            P("shard", ("ctx", "tp"), None),
            P("shard", ("ctx", "tp"), None),
            P("shard"),
            P("shard", "tp"),
            P("shard", None),
            P("shard", None),
            P("shard"),
            P("shard"),
            P("tp", "shard"),
            P("shard"),
            P("shard"),
            P("shard", "tp"),
            P("shard", "tp"),
            P("tp", "shard"),
            P("shard"),
        ),
        check_vma=False,
    )
```

```python
import functools
import math

import jax
import jax.numpy as jnp
from jax import lax
from jax.experimental import pallas as pl
from jax.experimental.pallas import tpu as pltpu
from jax.sharding import PartitionSpec as P

epsilon = 1e-06
rope_base = 1000000.0
gelu_coef = 0.044715
low = jnp.bfloat16
full = jnp.float32


def rms_scale(value):
    return lax.rsqrt(jnp.mean(value * value, axis=-1, keepdims=True) + epsilon)


def norm_back(grad_unit, unit, scale):
    return scale * (grad_unit - unit * jnp.mean(grad_unit * unit, axis=-1, keepdims=True))


def gelu_pair(value):
    root = math.sqrt(2.0 / math.pi)
    tangent = jnp.tanh(root * (value + gelu_coef * value * value * value))
    result = 0.5 * value * (1.0 + tangent)
    slope = 0.5 * (1.0 + tangent) + 0.5 * value * (1.0 - tangent * tangent) * root * (
        1.0 + 3.0 * gelu_coef * value * value
    )
    return (result, slope)


def rope_tables(places, width):
    half = width // 2
    freqs = rope_base ** (-(jnp.arange(half, dtype=full) * 2.0 / width))
    angles = places.astype(full)[:, None] * freqs[None, :]
    return (jnp.cos(angles), jnp.sin(angles))


def rotate(value, cosine, sine):
    half = value.shape[-1] // 2
    first = value[..., :half]
    second = value[..., half:]
    return jnp.concatenate(
        [first * cosine - second * sine, second * cosine + first * sine], axis=-1
    )


def unrotate(value, cosine, sine):
    return rotate(value, cosine, -sine)


def dot(left, right):
    return jnp.dot(left, right, preferred_element_type=full)


def dot_tn(left, right):
    return lax.dot_general(left, right, (((0,), (0,)), ((), ())), preferred_element_type=full)


def dot_nt(left, right):
    return lax.dot_general(left, right, (((1,), (1,)), ((), ())), preferred_element_type=full)


def pieces(value, axis):
    count = lax.axis_size(axis)
    return [value] + [
        lax.ppermute(value, axis, [(i, (i + o) % count) for i in range(count)])
        for o in range(1, count)
    ]


def gather_rows(value, axis):
    return jnp.concatenate(pieces(value, axis), axis=0)


def scatter_rows(value, axis):
    count = lax.axis_size(axis)
    rows = value.shape[0] // count
    total = value[:rows].astype(full)
    sent = value.astype(low)
    for o in range(1, count):
        block = sent[o * rows : (o + 1) * rows]
        total = total + lax.ppermute(
            block, axis, [(i, (i - o) % count) for i in range(count)]
        ).astype(full)
    return total


def shard_gather(value, dim):
    count = lax.axis_size("shard")
    if count != 2:
        return lax.all_gather(value, "shard", axis=dim, tiled=True)
    other = lax.ppermute(value, "shard", [(0, 1), (1, 0)])
    first = lax.axis_index("shard") == 0
    return jnp.concatenate(
        [jnp.where(first, value, other), jnp.where(first, other, value)], axis=dim
    )


def shard_scatter(value):
    count = lax.axis_size("shard")
    if count != 2:
        return lax.psum_scatter(value.astype(low), "shard", scatter_dimension=0, tiled=True)
    rows = value.shape[0] // 2
    me = lax.axis_index("shard")
    theirs = lax.dynamic_slice_in_dim(value, (1 - me) * rows, rows, 0).astype(low)
    mine = lax.dynamic_slice_in_dim(value, me * rows, rows, 0)
    return (
        mine.astype(full) + lax.ppermute(theirs, "shard", [(0, 1), (1, 0)]).astype(full)
    ).astype(low)


def axis_total(value, axis):
    count = lax.axis_size(axis)
    rows = value.shape[0] // count
    me = lax.axis_index(axis)
    total = None
    for o in range(count):
        block = lax.dynamic_slice_in_dim(value, ((me + o) % count) * rows, rows, 0)
        if o == 0:
            total = block.astype(full)
        else:
            total = total + lax.ppermute(
                block, axis, [(i, (i + o) % count) for i in range(count)]
            ).astype(full)
    return total.astype(low)


def axis_fill(chunk, axis):
    count = lax.axis_size(axis)
    rows = chunk.shape[0]
    me = lax.axis_index(axis)
    held = [chunk] + [
        lax.ppermute(chunk, axis, [(i, (i - o) % count) for i in range(count)])
        for o in range(1, count)
    ]
    twice = jnp.concatenate(held + held, axis=0)
    start = ((count - me) % count) * rows
    return lax.dynamic_slice_in_dim(twice, start, rows * count, 0)


def axis_sum(value, axis):
    total = None
    for piece in pieces(value, axis):
        total = piece.astype(full) if total is None else total + piece.astype(full)
    return total


def plain_body(
    hidden_in,
    positions,
    cotangent,
    input_gain,
    query_weight,
    key_weight,
    value_weight,
    query_gain,
    key_gain,
    out_weight,
    attn_post_gain,
    ffn_pre_gain,
    gate_weight,
    up_weight,
    down_weight,
    ffn_post_gain,
):
    width = hidden_in.shape[-1]
    head_dim = key_weight.shape[1]
    head_cols = query_weight.shape[1]
    hidden_cols = gate_weight.shape[1]
    heads = head_cols // head_dim
    factor = 1.0 / math.sqrt(head_dim)
    shards = lax.axis_size("shard")
    tps = lax.axis_size("tp")
    ctxs = lax.axis_size("ctx")
    own_in = hidden_in.reshape(-1, width)
    own_cot = cotangent.reshape(-1, width)
    part_rows = own_in.shape[0]
    me_tp = lax.axis_index("tp")

    rows_low = gather_rows(own_in, "tp")
    count = rows_low.shape[0]
    natural = positions.reshape(tps, part_rows)
    places = jnp.concatenate(
        [
            lax.dynamic_slice_in_dim(natural, (me_tp - o) % tps, 1, 0).reshape(-1)
            for o in range(tps)
        ]
    )
    places_all = gather_rows(places, "ctx")

    wide = width // shards
    slim = head_dim // shards
    packed = jnp.concatenate(
        [input_gain, attn_post_gain, ffn_pre_gain, ffn_post_gain, query_gain, key_gain]
    ).reshape(1, -1)
    gains = shard_gather(packed, 0).astype(full)

    def gain_at(start, size):
        return gains[:, start : start + size].reshape(-1)

    in_gain = gain_at(0, wide)
    post_gain = gain_at(wide, wide)
    pre_gain = gain_at(2 * wide, wide)
    last_gain = gain_at(3 * wide, wide)
    qgain = gain_at(4 * wide, slim)
    kgain = gain_at(4 * wide + slim, slim)
    qkv_full = shard_gather(jnp.concatenate([query_weight, key_weight, value_weight], axis=1), 0)
    query_full = qkv_full[:, :head_cols]
    key_full = qkv_full[:, head_cols : head_cols + head_dim]
    value_full = qkv_full[:, head_cols + head_dim :]
    out_full = shard_gather(out_weight, 1)
    gate_full = shard_gather(gate_weight, 0)
    up_full = shard_gather(up_weight, 0)
    down_full = shard_gather(down_weight, 1)

    rows = rows_low.astype(full)
    scale_in = rms_scale(rows)
    unit_in = rows * scale_in
    normed_in = (unit_in * in_gain).astype(low)
    cosine, sine = rope_tables(places, head_dim)
    key_raw = dot(normed_in, key_full)
    key_scale = rms_scale(key_raw)
    key_unit = key_raw * key_scale
    key_rot = rotate(key_unit * kgain, cosine, sine).astype(low)
    key_all = gather_rows(key_rot, "ctx")
    values = dot(normed_in, value_full).astype(low)
    value_all = gather_rows(values, "ctx")
    query_raw = dot(normed_in, query_full).reshape(count, heads, head_dim)
    query_scale = rms_scale(query_raw)
    query_unit = query_raw * query_scale
    query_rot = rotate(query_unit * qgain, cosine[:, None, :], sine[:, None, :]).astype(low)
    visible = places_all[None, None, :] <= places[None, :, None]
    scores = (
        jnp.einsum("qhd,kd->hqk", query_rot, key_all, preferred_element_type=full) * factor
    )
    weight = jnp.exp(jnp.where(visible, scores, -1e30))
    probs_full = weight * (1.0 / jnp.sum(weight, axis=-1, keepdims=True))
    probs = probs_full.astype(low)
    context3 = jnp.einsum(
        "hqk,kd->qhd", probs, value_all, preferred_element_type=full
    ).astype(low)
    context = context3.reshape(count, head_cols)
    attn_proj = scatter_rows(dot(context, out_full), "tp")

    own_rows = own_in.astype(full)
    grad_out = own_cot.astype(full)
    attn_scale = rms_scale(attn_proj)
    attn_unit = attn_proj * attn_scale
    resid = own_rows + attn_unit * post_gain
    ffn_scale = rms_scale(resid)
    ffn_unit = resid * ffn_scale
    ffn_rows = gather_rows((ffn_unit * pre_gain).astype(low), "tp")

    gate = dot(ffn_rows, gate_full)
    upper = dot(ffn_rows, up_full)
    gelu_val, gelu_slope = gelu_pair(gate)
    hidden_act = (gelu_val * upper).astype(low)
    ffn_proj = scatter_rows(dot(hidden_act, down_full), "tp")

    out_scale = rms_scale(ffn_proj)
    out_unit = ffn_proj * out_scale
    block_out = resid + out_unit * last_gain
    last_gain_grad = jnp.sum(grad_out * out_unit, axis=0)
    grad_proj_own = norm_back(grad_out * last_gain, out_unit, out_scale).astype(low)
    grad_proj_rows = gather_rows(grad_proj_own, "tp")

    grad_hidden = dot_nt(grad_proj_rows, down_full)
    grad_up = (grad_hidden * gelu_val).astype(low)
    grad_gate = (grad_hidden * upper * gelu_slope).astype(low)
    grad_ffn_in = scatter_rows(dot_nt(grad_gate, gate_full) + dot_nt(grad_up, up_full), "tp")

    pre_gain_grad = jnp.sum(grad_ffn_in * ffn_unit, axis=0)
    grad_resid = grad_out + norm_back(grad_ffn_in * pre_gain, ffn_unit, ffn_scale)
    post_gain_grad = jnp.sum(grad_resid * attn_unit, axis=0)
    grad_attn_own = norm_back(grad_resid * post_gain, attn_unit, attn_scale).astype(low)
    grad_attn_rows = gather_rows(grad_attn_own, "tp")

    early = shard_scatter(
        jnp.concatenate(
            [
                dot_tn(ffn_rows, grad_gate).astype(low),
                dot_tn(ffn_rows, grad_up).astype(low),
                dot_tn(grad_proj_rows, hidden_act).astype(low),
            ],
            axis=1,
        )
    )
    early_all = axis_fill(axis_total(early, "ctx"), "ctx")

    grad_context_flat = dot_nt(grad_attn_rows, out_full).astype(low)
    grad_context = grad_context_flat.reshape(count, heads, head_dim)
    delta = jnp.sum(grad_context.astype(full) * context3.astype(full), axis=-1)
    grad_probs = jnp.einsum("qhd,kd->hqk", grad_context, value_all, preferred_element_type=full)
    grad_scores = (probs_full * (grad_probs - delta.T[:, :, None]) * factor).astype(low)
    grad_key_part = jnp.einsum(
        "hqk,qhd->kd", grad_scores, query_rot, preferred_element_type=full
    ).astype(low)
    grad_value_part = jnp.einsum(
        "hqk,qhd->kd", probs, grad_context, preferred_element_type=full
    ).astype(low)
    grad_query_rot = jnp.einsum("hqk,kd->qhd", grad_scores, key_all, preferred_element_type=full)
    both = scatter_rows(jnp.concatenate([grad_key_part, grad_value_part], axis=1), "ctx")
    grad_key_rot = both[:, :head_dim]
    grad_value_low = both[:, head_dim:].astype(low)

    grad_query_gained = unrotate(grad_query_rot, cosine[:, None, :], sine[:, None, :])
    qgain_grad = jnp.sum(grad_query_gained * query_unit, axis=(0, 1))
    grad_query = (
        norm_back(grad_query_gained * qgain, query_unit, query_scale)
        .astype(low)
        .reshape(count, head_cols)
    )
    query_part = dot_nt(grad_query, query_full)

    grad_key_gained = unrotate(grad_key_rot, cosine, sine)
    kgain_grad = jnp.sum(grad_key_gained * key_unit, axis=0)
    grad_key = norm_back(grad_key_gained * kgain, key_unit, key_scale).astype(low)
    grad_normed_part = (
        query_part + dot_nt(grad_key, key_full) + dot_nt(grad_value_low, value_full)
    )
    in_gain_grad = jnp.sum(grad_normed_part * unit_in, axis=0)
    grad_normed = scatter_rows(grad_normed_part, "tp")
    own_scale = rms_scale(own_rows)
    hidden_grad = grad_resid + norm_back(grad_normed * in_gain, own_rows * own_scale, own_scale)

    small_width = 2 * head_dim
    late_q = jnp.concatenate(
        [
            dot_tn(normed_in, grad_query).astype(low),
            dot_tn(grad_attn_rows, context).astype(low),
        ],
        axis=1,
    )
    late_kv = jnp.concatenate(
        [
            dot_tn(normed_in, grad_key).astype(low),
            dot_tn(normed_in, grad_value_low).astype(low),
        ],
        axis=1,
    )
    vectors = jnp.concatenate(
        [
            item.reshape(shards, -1)
            for item in (
                in_gain_grad,
                post_gain_grad,
                pre_gain_grad,
                last_gain_grad,
                qgain_grad,
                kgain_grad,
            )
        ],
        axis=1,
    ).astype(low)
    length = vectors.shape[1]
    late_q_own = axis_total(shard_scatter(late_q), "ctx")
    late_kv_own = axis_total(shard_scatter(late_kv), "ctx")
    late_kv_own = axis_sum(late_kv_own, "tp").astype(low)
    late_all = axis_fill(jnp.concatenate([late_q_own, late_kv_own], axis=1), "ctx").astype(full)
    vector_own = shard_scatter(vectors.reshape(shards, 1, length)).reshape(1, length)
    vector_own = axis_sum(axis_sum(vector_own, "ctx").astype(low), "tp").reshape(length)

    def vector_at(start, size):
        return vector_own[start : start + size]

    early_all = early_all.astype(full)
    gate_grad = early_all[:, :hidden_cols]
    up_grad = early_all[:, hidden_cols : 2 * hidden_cols]
    down_grad = early_all[:, 2 * hidden_cols :].T
    query_grad = late_all[:, :head_cols]
    out_grad = late_all[:, head_cols : 2 * head_cols].T
    key_grad = late_all[:, 2 * head_cols : 2 * head_cols + head_dim]
    value_grad = late_all[:, 2 * head_cols + head_dim :]
    return (
        block_out.reshape(hidden_in.shape),
        hidden_grad.reshape(hidden_in.shape),
        vector_at(0, wide),
        query_grad,
        key_grad,
        value_grad,
        vector_at(4 * wide, slim),
        vector_at(4 * wide + slim, slim),
        out_grad,
        vector_at(wide, wide),
        vector_at(2 * wide, wide),
        gate_grad,
        up_grad,
        down_grad,
        vector_at(3 * wide, wide),
    )


def run(kernel, outs, *args, scalars=None, scratch=()):
    vmem = pl.BlockSpec(memory_space=pltpu.VMEM)
    specs = [vmem] * len(args)
    if scalars is not None:
        specs = [pl.BlockSpec(memory_space=pltpu.SMEM)] + specs
        args = (scalars,) + args
    return pl.pallas_call(
        kernel,
        out_shape=[jax.ShapeDtypeStruct(shape, kind) for shape, kind in outs],
        in_specs=specs,
        out_specs=[vmem] * len(outs),
        scratch_shapes=list(scratch),
        compiler_params=pltpu.CompilerParams(vmem_limit_bytes=24 * 1024 * 1024),
    )(*args)


def store_blocks(value, refs):
    rows = refs[0].shape[0]
    for o, ref in enumerate(refs):
        ref[...] = value[o * rows : (o + 1) * rows].astype(ref.dtype)


def total_of(refs):
    total = refs[0][...].astype(full)
    for ref in refs[1:]:
        total = total + ref[...].astype(full)
    return total


def unit_of(value):
    scale = rms_scale(value)
    return value * scale, scale


def query_kernel(rows, gd, gh, cos, sin, wq, wk, wv, q_rot, q_unit, q_scale, k_rot, val):
    unit, _ = unit_of(rows[...].astype(full))
    normed = (unit * gd[0:1, :]).astype(low)
    key_unit, _ = unit_of(dot(normed, wk[...]))
    k_rot[...] = rotate(key_unit * gh[1:2, :], cos[...], sin[...]).astype(low)
    val[...] = dot(normed, wv[...]).astype(low)
    query_unit, query_scale = unit_of(dot(normed, wq[...]))
    q_unit[...] = query_unit
    q_scale[...] = query_scale
    q_rot[...] = rotate(query_unit * gh[0:1, :], cos[...], sin[...]).astype(low)


def attend_kernel(n, *refs):
    q_rot, k_own, v_own = refs[:3]
    others = refs[3 : 2 + n]
    gd, gh, cos, sin, wk, wv, wot, at_query, at_key = refs[2 + n : 11 + n]
    k_all, v_all, context, probs = refs[11 + n : 15 + n]
    blocks = refs[15 + n :]
    rows = k_own.shape[0]
    k_all[0:rows, :] = k_own[...]
    v_all[0:rows, :] = v_own[...]
    for o, other in enumerate(others, 1):
        at = slice(o * rows, (o + 1) * rows)
        unit, _ = unit_of(other[...].astype(full))
        normed = (unit * gd[0:1, :]).astype(low)
        key_unit, _ = unit_of(dot(normed, wk[...]))
        k_all[at, :] = rotate(key_unit * gh[1:2, :], cos[at, :], sin[at, :]).astype(low)
        v_all[at, :] = dot(normed, wv[...]).astype(low)
    factor = 1.0 / math.sqrt(q_rot.shape[1])
    scores = dot_nt(q_rot[...], k_all[...]) * factor
    weight = jnp.exp(jnp.where(at_key[...] <= at_query[...], scores, -1e30))
    chance = weight * (1.0 / jnp.sum(weight, axis=-1, keepdims=True))
    probs[...] = chance
    mixed = dot(chance.astype(low), v_all[...]).astype(low)
    context[...] = mixed
    store_blocks(dot_nt(mixed, wot[...]), blocks)


def middle_kernel(b0, b1, b2, b3, own_in, gd, attn_proj, ffn_own):
    proj = total_of((b0, b1, b2, b3))
    attn_proj[...] = proj
    attn_unit, _ = unit_of(proj)
    ffn_unit, _ = unit_of(own_in[...].astype(full) + attn_unit * gd[1:2, :])
    ffn_own[...] = (ffn_unit * gd[2:3, :]).astype(low)


def ffn_kernel(f0, f1, f2, f3, wg, wu, wdt, ffn_rows, gate, upper, act, *blocks):
    rows = f0.shape[0]
    for o, ref in enumerate((f0, f1, f2, f3)):
        ffn_rows[o * rows : (o + 1) * rows, :] = ref[...]
    held = ffn_rows[...]
    gate_val = dot(held, wg[...])
    upper_val = dot(held, wu[...])
    gate[...] = gate_val
    upper[...] = upper_val
    gelu_val, _ = gelu_pair(gate_val)
    hidden = (gelu_val * upper_val).astype(low)
    act[...] = hidden
    store_blocks(dot_nt(hidden, wdt[...]), blocks)


def turn_kernel(b0, b1, b2, b3, own_in, attn_proj, cot, gd, block_out, grad_own, last_grad):
    out_unit, out_scale = unit_of(total_of((b0, b1, b2, b3)))
    attn_unit, _ = unit_of(attn_proj[...])
    grad_out = cot[...].astype(full)
    grad_own[...] = norm_back(grad_out * gd[3:4, :], out_unit, out_scale).astype(low)
    resid = own_in[...].astype(full) + attn_unit * gd[1:2, :]
    block_out[...] = resid + out_unit * gd[3:4, :]
    last_grad[...] = jnp.sum(grad_out * out_unit, axis=0, keepdims=True)


def ffn_back_kernel(g0, g1, g2, g3, gate, upper, wg, wu, wdt, g_rows, g_gate, g_up, *blocks):
    rows = g0.shape[0]
    for o, ref in enumerate((g0, g1, g2, g3)):
        g_rows[o * rows : (o + 1) * rows, :] = ref[...]
    grad_hidden = dot(g_rows[...], wdt[...])
    gelu_val, gelu_slope = gelu_pair(gate[...])
    grad_up = (grad_hidden * gelu_val).astype(low)
    grad_gate = (grad_hidden * upper[...] * gelu_slope).astype(low)
    g_up[...] = grad_up
    g_gate[...] = grad_gate
    store_blocks(dot_nt(grad_gate, wg[...]) + dot_nt(grad_up, wu[...]), blocks)


def store_halves(first, theirs, mine, at, value):
    half = value.shape[0] // 2
    value = value.astype(low)
    mine[:, at] = jnp.where(first, value[:half], value[half:])
    theirs[:, at] = jnp.where(first, value[half:], value[:half])


def early_kernel(place, ffn_rows, g_rows, g_gate, g_up, act, theirs, mine):
    first = place[0] == 0
    cols = g_gate.shape[1]
    held = ffn_rows[...]
    store_halves(first, theirs, mine, slice(0, cols), dot_tn(held, g_gate[...]))
    store_halves(first, theirs, mine, slice(cols, 2 * cols), dot_tn(held, g_up[...]))
    store_halves(first, theirs, mine, slice(2 * cols, 3 * cols), dot_tn(g_rows[...], act[...]))


def chunk_kernel(place, mine, came, *chunks):
    n = len(chunks)
    rows = chunks[0].shape[0]
    for o, chunk in enumerate(chunks):
        start = pl.multiple_of(lax.rem(place[1] + o, n) * rows, 16)
        chunk[...] = (
            mine[pl.ds(start, rows), :].astype(full) + came[pl.ds(start, rows), :].astype(full)
        ).astype(chunk.dtype)


def sum_kernel(*refs):
    refs[-1][...] = total_of(refs[:-1]).astype(refs[-1].dtype)


def split_sum_kernel(*refs):
    total = total_of(refs[:-2]).astype(low)
    half = refs[-1].shape[1]
    refs[-2][...] = total[:, :half]
    refs[-1][...] = total[:, half:]


def join_sum_kernel(left, *refs):
    half = left.shape[1]
    refs[-1][:, :half] = left[...]
    refs[-1][:, half:] = total_of(refs[:-1]).astype(low)


def early_out_kernel(place, c0, c1, c2, c3, gate_grad, up_grad, down_turned):
    rows = c0.shape[0]
    cols = gate_grad.shape[1]
    for o, chunk in enumerate((c0, c1, c2, c3)):
        start = pl.multiple_of(lax.rem(place[1] + o, 4) * rows, 16)
        value = chunk[...].astype(full)
        gate_grad[pl.ds(start, rows), :] = value[:, :cols]
        up_grad[pl.ds(start, rows), :] = value[:, cols : 2 * cols]
        down_turned[pl.ds(start, rows), :] = value[:, 2 * cols :]


def late_out_kernel(place, c0, c1, c2, c3, query_grad, out_turned, key_grad, value_grad, vector):
    rows = query_grad.shape[0] // 4
    cols = query_grad.shape[1]
    for o, chunk in enumerate((c0, c1, c2, c3)):
        which = lax.rem(place[1] + o, 4)
        start = pl.multiple_of(which * rows, 16)
        value = chunk[0:rows, :].astype(full)
        query_grad[pl.ds(start, rows), :] = value[:, :cols]
        out_turned[pl.ds(start, rows), :] = value[:, cols : 2 * cols]
        key_grad[pl.ds(start, rows), :] = value[:, 2 * cols : 3 * cols]
        value_grad[pl.ds(start, rows), :] = value[:, 3 * cols :]
        tail = chunk[rows:, 2 * cols :].astype(full)
        vector[pl.ds(pl.multiple_of(which * 8, 8), 8), :] = tail[0:8, :]


def grad_middle_kernel(
    b0, b1, b2, b3, own_in, attn_proj, cot, gd, grad_resid, grad_own, pre_grad, post_grad
):
    grad_ffn_in = total_of((b0, b1, b2, b3))
    attn_unit, attn_scale = unit_of(attn_proj[...])
    ffn_unit, ffn_scale = unit_of(own_in[...].astype(full) + attn_unit * gd[1:2, :])
    resid_grad = cot[...].astype(full) + norm_back(
        grad_ffn_in * gd[2:3, :], ffn_unit, ffn_scale
    )
    grad_own[...] = norm_back(resid_grad * gd[1:2, :], attn_unit, attn_scale).astype(low)
    grad_resid[...] = resid_grad
    pre_grad[...] = jnp.sum(grad_ffn_in * ffn_unit, axis=0, keepdims=True)
    post_grad[...] = jnp.sum(resid_grad * attn_unit, axis=0, keepdims=True)


def attend_back_kernel(
    a0, a1, a2, a3, wot, context, probs, q_rot, k_all, v_all, a_rows, grad_query, *blocks
):
    rows = a0.shape[0]
    for o, ref in enumerate((a0, a1, a2, a3)):
        a_rows[o * rows : (o + 1) * rows, :] = ref[...]
    grad_context = dot(a_rows[...], wot[...]).astype(low)
    delta = jnp.sum(
        grad_context.astype(full) * context[...].astype(full), axis=-1, keepdims=True
    )
    factor = 1.0 / math.sqrt(q_rot.shape[1])
    chance = probs[...]
    grad_probs = dot_nt(grad_context, v_all[...])
    grad_scores = (chance * (grad_probs - delta) * factor).astype(low)
    keys = dot_tn(grad_scores, q_rot[...]).astype(low)
    vals = dot_tn(chance.astype(low), grad_context).astype(low)
    size = blocks[0].shape[0]
    wide = keys.shape[1]
    for o, block in enumerate(blocks):
        block[:, :wide] = keys[o * size : (o + 1) * size]
        block[:, wide:] = vals[o * size : (o + 1) * size]
    grad_query[...] = dot(grad_scores, k_all[...])


def late_kernel(
    place, grad_rot, q_unit, q_scale, gd, gh, cos, sin, wq, wk, wv, a_rows, context,
    g0, g1, g2, g3, h0, h1, h2, h3, post_grad, pre_grad, last_grad,
    theirs, mine, query_part,
):
    first = place[0] == 0
    size = h0.shape[0]
    gained = unrotate(grad_rot[...], cos[0:size, :], sin[0:size, :])
    query_unit = q_unit[...]
    qgain_grad = jnp.sum(gained * query_unit, axis=0, keepdims=True)
    grad_query = norm_back(gained * gh[0:1, :], query_unit, q_scale[...]).astype(low)
    q_part = dot_nt(grad_query, wq[...])
    query_part[...] = q_part
    cols = grad_query.shape[1]
    kgain_grad = jnp.zeros_like(qgain_grad)
    in_grad = None
    key_weight = None
    for o, (held, grads) in enumerate(((h0, g0), (h1, g1), (h2, g2), (h3, g3))):
        at = slice(o * size, (o + 1) * size)
        unit, _ = unit_of(held[...].astype(full))
        normed = (unit * gd[0:1, :]).astype(low)
        key_unit, key_scale = unit_of(dot(normed, wk[...]))
        gained = unrotate(grads[:, :cols].astype(full), cos[at, :], sin[at, :])
        kgain_grad = kgain_grad + jnp.sum(gained * key_unit, axis=0, keepdims=True)
        grad_key = norm_back(gained * gh[1:2, :], key_unit, key_scale).astype(low)
        grad_value = grads[:, cols:]
        part = dot_nt(grad_key, wk[...]) + dot_nt(grad_value, wv[...])
        if o == 0:
            part = part + q_part
            query_weight = dot_tn(normed, grad_query)
            key_weight = dot_tn(normed, grad_key)
            value_weight = dot_tn(normed, grad_value)
            in_grad = jnp.sum(part * unit, axis=0, keepdims=True)
        else:
            key_weight = key_weight + dot_tn(normed, grad_key)
            value_weight = value_weight + dot_tn(normed, grad_value)
            in_grad = in_grad + jnp.sum(part * unit, axis=0, keepdims=True)
    out_weight = dot_tn(a_rows[...], context[...])
    half = query_weight.shape[0] // 2
    rows = half // 4
    stride = rows + 16
    slim = cols // 2
    weights = [w.astype(low) for w in (query_weight, out_weight, key_weight, value_weight)]
    wide_vectors = (in_grad, post_grad[...], pre_grad[...], last_grad[...])
    sides = [
        jnp.concatenate(
            [v[:, s * half : (s + 1) * half] for v in wide_vectors]
            + [v[:, s * slim : (s + 1) * slim] for v in (qgain_grad, kgain_grad)],
            axis=1,
        )
        for s in range(2)
    ]
    length = sides[0].shape[1] // 4
    for target, pick in ((mine, 0), (theirs, 1)):
        vector = jnp.where(first, sides[pick], sides[1 - pick])
        for j, w in enumerate(weights):
            chosen = jnp.where(
                first,
                w[pick * half : (pick + 1) * half],
                w[(1 - pick) * half : (2 - pick) * half],
            )
            for c in range(4):
                target[c * stride : c * stride + rows, j * cols : (j + 1) * cols] = chosen[
                    c * rows : (c + 1) * rows
                ]
        for c in range(4):
            tail = slice(c * stride + rows, (c + 1) * stride)
            target[tail, :] = jnp.zeros((16, target.shape[1]), low)
            target[tail, 2 * cols : 2 * cols + length] = jnp.broadcast_to(
                vector[:, c * length : (c + 1) * length], (16, length)
            ).astype(low)


def join_kernel(g0, g1, g2, g3, rows, gd, gh, cos, sin, wk, wv, query_part, *blocks):
    grads = total_of((g0, g1, g2, g3))
    cols = wk.shape[1]
    unit, _ = unit_of(rows[...].astype(full))
    normed = (unit * gd[0:1, :]).astype(low)
    key_unit, key_scale = unit_of(dot(normed, wk[...]))
    gained = unrotate(grads[:, :cols], cos[...], sin[...])
    grad_key = norm_back(gained * gh[1:2, :], key_unit, key_scale).astype(low)
    part = query_part[...] + dot_nt(grad_key, wk[...])
    store_blocks(part + dot_nt(grads[:, cols:].astype(low), wv[...]), blocks)


def final_kernel(b0, b1, b2, b3, own_in, grad_resid, gd, hidden_grad):
    unit, scale = unit_of(own_in[...].astype(full))
    grad = total_of((b0, b1, b2, b3))
    hidden_grad[...] = grad_resid[...] + norm_back(grad * gd[0:1, :], unit, scale)


def send(value, axis, offset, name):
    count = lax.axis_size(axis)
    with jax.named_scope(name):
        return lax.ppermute(value, axis, [(i, (i + offset) % count) for i in range(count)])


def spread(value, axis, name):
    return [value] + [send(value, axis, o, f"{name}_{o}") for o in range(1, lax.axis_size(axis))]


def deal(blocks, axis, name):
    return [blocks[0]] + [send(b, axis, -o, f"{name}_{o}") for o, b in enumerate(blocks) if o]


def deal_up(blocks, axis, name):
    return [blocks[0]] + [send(b, axis, o, f"{name}_{o}") for o, b in enumerate(blocks) if o]


def pair_gather(value, name):
    other = send(value, "shard", 1, name)
    first = lax.axis_index("shard") == 0
    return jnp.concatenate(
        [jnp.where(first, value, other), jnp.where(first, other, value)], axis=0
    )


def body(
    hidden_in,
    positions,
    cotangent,
    input_gain,
    query_weight,
    key_weight,
    value_weight,
    query_gain,
    key_gain,
    out_weight,
    attn_post_gain,
    ffn_pre_gain,
    gate_weight,
    up_weight,
    down_weight,
    ffn_post_gain,
):
    width = hidden_in.shape[-1]
    head_dim = key_weight.shape[1]
    cols = gate_weight.shape[1]
    tps = lax.axis_size("tp")
    ctxs = lax.axis_size("ctx")
    own_in = hidden_in.reshape(-1, width)
    cot = cotangent.reshape(-1, width)
    part = own_in.shape[0]
    count = part * tps
    me_tp = lax.axis_index("tp")
    place = jnp.stack([lax.axis_index("shard"), lax.axis_index("ctx")]).astype(jnp.int32)

    rows = jnp.concatenate(spread(own_in, "tp", "rows"), axis=0)
    natural = positions.reshape(tps, part)
    places = jnp.concatenate(
        [lax.dynamic_slice_in_dim(natural, (me_tp - o) % tps, 1, 0) for o in range(tps)], axis=1
    )
    places_all = jnp.concatenate(spread(places, "ctx", "places"), axis=1).astype(full)
    cos, sin = rope_tables(places_all.reshape(-1), head_dim)
    at_query = places.astype(full).reshape(count, 1)

    wide = width // 2
    slim = head_dim // 2
    query_full = pair_gather(query_weight, "wq")
    key_full = pair_gather(key_weight, "wk")
    value_full = pair_gather(value_weight, "wv")
    packed = jnp.concatenate(
        [input_gain, attn_post_gain, ffn_pre_gain, ffn_post_gain, query_gain, key_gain]
    ).reshape(1, -1)
    gains = pair_gather(packed, "gains").astype(full)
    gd = gains[:, : 4 * wide].reshape(2, 4, wide).transpose(1, 0, 2).reshape(4, width)
    gh = gains[:, 4 * wide :].reshape(2, 2, slim).transpose(1, 0, 2).reshape(2, head_dim)
    out_turned = pair_gather(out_weight.T, "wo")
    gate_full = pair_gather(gate_weight, "wg")
    up_full = pair_gather(up_weight, "wu")
    down_turned = pair_gather(down_weight.T, "wd")

    block_outs = [((part, width), full)] + [((part, width), low)] * (tps - 1)
    held = spread(rows, "ctx", "held")
    q_rot, q_unit, q_scale, k_own, v_own = run(
        query_kernel,
        [
            ((count, head_dim), low),
            ((count, head_dim), full),
            ((count, 1), full),
            ((count, head_dim), low),
            ((count, head_dim), low),
        ],
        rows, gd, gh, cos[:count], sin[:count], query_full, key_full, value_full,
    )
    k_all, v_all, context, probs, *blocks = run(
        functools.partial(attend_kernel, ctxs),
        [
            ((ctxs * count, head_dim), low),
            ((ctxs * count, head_dim), low),
            ((count, head_dim), low),
            ((count, ctxs * count), full),
        ]
        + block_outs,
        q_rot, k_own, v_own, *held[1:], gd, gh, cos, sin, key_full, value_full, out_turned,
        at_query, places_all,
    )
    blocks = deal(blocks, "tp", "attn_rs")
    attn_proj, ffn_own = run(
        middle_kernel, [((part, width), full), ((part, width), low)], *blocks, own_in, gd
    )
    ffn_rows, gate, upper, act, *blocks = run(
        ffn_kernel,
        [
            ((count, width), low),
            ((count, cols), full),
            ((count, cols), full),
            ((count, cols), low),
        ]
        + block_outs,
        *spread(ffn_own, "tp", "ffn_ag"), gate_full, up_full, down_turned,
    )
    blocks = deal(blocks, "tp", "ffn_rs")
    block_out, grad_own, last_grad = run(
        turn_kernel,
        [((part, width), full), ((part, width), low), ((1, width), full)],
        *blocks, own_in, attn_proj, cot, gd,
    )
    g_rows, g_gate, g_up, *blocks = run(
        ffn_back_kernel,
        [((count, width), low), ((count, cols), low), ((count, cols), low)] + block_outs,
        *spread(grad_own, "tp", "gproj_ag"), gate, upper, gate_full, up_full, down_turned,
    )
    blocks = deal(blocks, "tp", "gffn_rs")

    theirs, mine = run(
        early_kernel,
        [((wide, 3 * cols), low)] * 2,
        ffn_rows, g_rows, g_gate, g_up, act, scalars=place,
    )
    came = send(theirs, "shard", 1, "early_pair")
    chunk = wide // ctxs
    chunks = run(
        chunk_kernel,
        [((chunk, 3 * cols), full)] + [((chunk, 3 * cols), low)] * (ctxs - 1),
        mine, came, scalars=place,
    )
    chunks = deal_up(chunks, "ctx", "early_rs")

    grad_resid, attn_grad_own, pre_grad, post_grad = run(
        grad_middle_kernel,
        [((part, width), full), ((part, width), low), ((1, width), full), ((1, width), full)],
        *blocks, own_in, attn_proj, cot, gd,
    )
    attn_pieces = spread(attn_grad_own, "tp", "gattn_ag")
    (early_total,) = run(sum_kernel, [((chunk, 3 * cols), low)], *chunks)
    early_all = deal([early_total] * ctxs, "ctx", "early_ag")

    a_rows, grad_rot, *grads = run(
        attend_back_kernel,
        [((count, width), low), ((count, head_dim), full)]
        + [((count, 2 * head_dim), low)] * ctxs,
        *attn_pieces, out_turned, context, probs, q_rot, k_all, v_all,
    )
    dealt = deal(grads, "ctx", "gkv_rs")
    late_rows = wide + 16 * ctxs
    theirs, mine, query_part = run(
        late_kernel,
        [((late_rows, 4 * head_dim), low)] * 2 + [((count, width), full)],
        grad_rot, q_unit, q_scale, gd, gh, cos, sin, query_full, key_full, value_full,
        a_rows, context, *grads, *held, post_grad, pre_grad, last_grad,
        scalars=place,
    )
    came = send(theirs, "shard", 1, "late_pair")
    chunks = run(
        chunk_kernel,
        [((late_rows // ctxs, 4 * head_dim), full)]
        + [((late_rows // ctxs, 4 * head_dim), low)] * (ctxs - 1),
        mine, came, scalars=place,
    )
    chunks = deal_up(chunks, "ctx", "late_rs")

    blocks = run(
        join_kernel,
        block_outs,
        *dealt, rows, gd, gh, cos[:count], sin[:count], key_full, value_full, query_part,
    )
    blocks = deal(blocks, "tp", "hidden_rs")
    left, right = run(
        split_sum_kernel, [((late_rows // ctxs, 2 * head_dim), low)] * 2, *chunks
    )
    rights = spread(right, "tp", "late_z")
    (hidden_grad,) = run(final_kernel, [((part, width), full)], *blocks, own_in, grad_resid, gd)
    (late_total,) = run(
        join_sum_kernel, [((late_rows // ctxs, 4 * head_dim), low)], left, *rights
    )
    late_all = deal([late_total] * ctxs, "ctx", "late_ag")

    gate_grad, up_grad, down_grad = run(
        early_out_kernel, [((wide, cols), full)] * 3, *early_all, scalars=place
    )
    query_grad, out_grad, key_grad, value_grad, vector = run(
        late_out_kernel,
        [((wide, head_dim), full)] * 4 + [((8 * ctxs, 2 * head_dim), full)],
        *late_all, scalars=place,
    )
    length = (4 * wide + 2 * slim) // ctxs
    vector = vector.reshape(ctxs, 8, 2 * head_dim)[:, 0, :length].reshape(-1)

    def vector_at(start, size):
        return vector[start : start + size]

    return (
        block_out.reshape(hidden_in.shape),
        hidden_grad.reshape(hidden_in.shape),
        vector_at(0, wide),
        query_grad,
        key_grad,
        value_grad,
        vector_at(4 * wide, slim),
        vector_at(4 * wide + slim, slim),
        out_grad.T,
        vector_at(wide, wide),
        vector_at(2 * wide, wide),
        gate_grad,
        up_grad,
        down_grad.T,
        vector_at(3 * wide, wide),
    )


def chosen_body(mesh):
    def pick(*args):
        width = args[0].shape[-1]
        fits = (
            mesh.shape["shard"] == 2
            and mesh.shape["ctx"] == 4
            and mesh.shape["tp"] == 4
            and args[4].shape[1] == args[5].shape[1]
            and (width // 8) % 16 == 0
        )
        return (body if fits else plain_body)(*args)

    return pick


def solution(mesh):
    placed = (
        P("shard", ("ctx", "tp"), None),
        P("shard", "ctx"),
        P("shard", ("ctx", "tp"), None),
        P("shard"),
        P("shard", "tp"),
        P("shard", None),
        P("shard", None),
        P("shard"),
        P("shard"),
        P("tp", "shard"),
        P("shard"),
        P("shard"),
        P("shard", "tp"),
        P("shard", "tp"),
        P("tp", "shard"),
        P("shard"),
    )
    return jax.shard_map(
        chosen_body(mesh),
        mesh=mesh,
        in_specs=placed,
        out_specs=(
            P("shard", ("ctx", "tp"), None),
            P("shard", ("ctx", "tp"), None),
            P("shard"),
            P("shard", "tp"),
            P("shard", None),
            P("shard", None),
            P("shard"),
            P("shard"),
            P("tp", "shard"),
            P("shard"),
            P("shard"),
            P("shard", "tp"),
            P("shard", "tp"),
            P("tp", "shard"),
            P("shard"),
        ),
        check_vma=False,
    )
```
